256 devices in a mesh: gx: 8 (over x, z_lo), gy: 32 (over y, z_hi, core).
Axes of the slice: x: 4, y: 4, z: 8 (z_hi: 4, z_lo: 2; z = z_hi * 2 + z_lo), core: 2. Of those that a mesh axis runs over, the one named last changes fastest.
Arguments:
- tokens: bfloat16 [512, 16384], P('gy', 'gx'), may hold values from -6 to 6
- gate_weight: bfloat16 [16384, 28672], P('gx', 'gy'), may hold values from -0.046875 to 0.046875
- up_weight: bfloat16 [16384, 28672], P('gx', 'gy'), may hold values from -0.046875 to 0.046875
- down_weight: bfloat16 [28672, 16384], P('gy', 'gx'), may hold values from -0.03125 to 0.03125
Outputs:
- mixed: bfloat16 [512, 16384], P('gy', 'gx')
The draws below stay inside these ranges and needn't reach their ends.
All inputs are finite; a program needn't handle non-finite values.
Results may differ from the reference program's by a relative error of at most 0.025.
Values may be sent and summed in bfloat16 or wider, within the bound.
No kernel may reach another device: no remote copies, remote signals or barrier semaphores. Data moves between devices by JAX's collectives and lax.ppermute only.
A program may use at most 64 MiB of HBM per device.

```python
import jax
import jax.numpy as jnp
from jax import lax

D = 16384
FF = 28672
TOKENS = 512
N_GX = 8
N_GY = 32


def level_of(own_key, dims, split, least, top_value):
    def one(position, shards_of):
        heights = jax.random.uniform(jax.random.fold_in(jax.random.fold_in(own_key, 6), position), (shards_of,), jnp.float32, least / len(split), top_value / len(split))
        return jnp.repeat(jnp.exp(heights), dims[position] // shards_of).reshape((-1,) + (1,) * (len(dims) - position - 1))

    loudness = one(*split[0])
    for cut in split[1:]:
        loudness = loudness * one(*cut)
    return loudness


def centred(stream_key, dims, spread, most, shards=(), dtype=jnp.bfloat16):
    drawn = spread * jax.random.normal(stream_key, dims, jnp.float32)
    if shards:
        drawn = drawn * level_of(stream_key, dims, shards, -0.22, 0.18)
    return jnp.clip(drawn, -most, most).astype(dtype)


def setup_inputs(seed: int = 0) -> dict:
    seeds = jax.random.split(jax.random.key(seed), 5)
    return {
        "tokens": centred(seeds[0], (TOKENS, D), 1.0, 6.0, ((0, 32), (1, 8))),
        "gate_weight": centred(seeds[1], (D, FF), D ** -0.5, 0.046875, ((0, 8), (1, 32))),
        "up_weight": centred(seeds[2], (D, FF), D ** -0.5, 0.046875, ((0, 8), (1, 32))),
        "down_weight": centred(seeds[3], (FF, D), FF ** -0.5, 0.03125, ((0, 32), (1, 8))),
    }


def rounded(value):
    return lax.optimization_barrier(value.astype(jnp.bfloat16)).astype(jnp.float32)


def reference(tokens, gate_weight, up_weight, down_weight):
    rows_all = tokens.shape[0]
    block_width = D // N_GX
    gate = jnp.zeros((rows_all, FF), jnp.float32)
    up = jnp.zeros((rows_all, FF), jnp.float32)
    for block in range(N_GX):
        lo_col = block * block_width
        piece = tokens[:, lo_col:lo_col + block_width]
        gate = gate + rounded(jnp.dot(piece, gate_weight[lo_col:lo_col + block_width], preferred_element_type=jnp.float32))
        up = up + rounded(jnp.dot(piece, up_weight[lo_col:lo_col + block_width], preferred_element_type=jnp.float32))
    hidden = (jax.nn.silu(gate) * up).astype(jnp.bfloat16)
    span = FF // N_GY
    mixed = jnp.zeros((rows_all, D), jnp.float32)
    for block in range(N_GY):
        lo_row = block * span
        mixed = mixed + rounded(jnp.dot(hidden[:, lo_row:lo_row + span], down_weight[lo_row:lo_row + span], preferred_element_type=jnp.float32))
    return mixed.astype(jnp.bfloat16)
```

```python
import jax
import jax.numpy as jnp
from jax import lax
from jax.sharding import PartitionSpec as P

CORES, Z_PARTS, Y_PARTS = 2, 4, 4


def swap(value, step):
    size = CORES * Z_PARTS * Y_PARTS
    return lax.ppermute(value, "gy", [(a, a ^ step) for a in range(size)])


def gather_steps(value, unit, parts):
    return jnp.concatenate([value] + [swap(value, unit * i) for i in range(1, parts)], 0)


def reduce_steps(value, unit, parts):
    rows = value.shape[0] // parts
    pieces = [value[i * rows:(i + 1) * rows] for i in range(parts)]
    total = pieces[0].astype(jnp.float32)
    for i in range(1, parts):
        total = total + swap(pieces[i], unit * i).astype(jnp.float32)
    return total.astype(jnp.bfloat16)


def per_device(tokens, gate_weight, up_weight, down_weight):
    width = gate_weight.shape[1]
    groups = lax.axis_size("gx")
    both = jnp.concatenate([gate_weight, up_weight], 1)
    part = gather_steps(tokens, CORES, Z_PARTS)
    part = gather_steps(part, CORES * Z_PARTS, Y_PARTS)
    part = gather_steps(part, 1, CORES)
    term = jnp.dot(part, both, preferred_element_type=jnp.float32).astype(jnp.bfloat16)
    rows = term.shape[0] // groups
    terms = lax.all_to_all(term.reshape(groups, rows, 2 * width), "gx", 0, 0)
    summed = terms.astype(jnp.float32).sum(0)
    hidden_part = (jax.nn.silu(summed[:, :width]) * summed[:, width:]).astype(jnp.bfloat16)
    hidden = lax.all_to_all(
        jnp.broadcast_to(hidden_part[None], (groups, rows, width)), "gx", 0, 0
    ).reshape(groups * rows, width)
    half = hidden.shape[0] // 2
    theirs = jnp.dot(hidden[half:], down_weight, preferred_element_type=jnp.float32).astype(jnp.bfloat16)
    came = swap(theirs, 1)
    mine = jnp.dot(hidden[:half], down_weight, preferred_element_type=jnp.float32)
    out = (mine + came.astype(jnp.float32)).astype(jnp.bfloat16)
    out = reduce_steps(out, CORES * Z_PARTS, Y_PARTS)
    return reduce_steps(out, CORES, Z_PARTS)


def solution(mesh):
    in_specs = (P("gy", "gx"), P("gx", "gy"), P("gx", "gy"), P("gy", "gx"))
    out_specs = P("gy", "gx")
    return jax.shard_map(
        per_device, mesh=mesh, in_specs=in_specs, out_specs=out_specs, check_vma=False
    )
```

```python
import jax
import jax.numpy as jnp
from jax import lax
from jax.sharding import PartitionSpec as P

CORES, Z_PARTS, Y_PARTS = 2, 4, 4
CHUNKS = 2


def swap(value, step):
    size = CORES * Z_PARTS * Y_PARTS
    return lax.ppermute(value, "gy", [(a, a ^ step) for a in range(size)])


def gather_steps(value, unit, parts):
    return jnp.concatenate([value] + [swap(value, unit * i) for i in range(1, parts)], 0)


def reduce_steps(value, unit, parts):
    rows = value.shape[0] // parts
    pieces = [value[i * rows:(i + 1) * rows] for i in range(parts)]
    total = pieces[0].astype(jnp.float32)
    for i in range(1, parts):
        total = total + swap(pieces[i], unit * i).astype(jnp.float32)
    return total.astype(jnp.bfloat16)


def after(value, *others):
    return lax.optimization_barrier((value,) + others)[0]


def dot(left, right):
    return jnp.dot(left, right, preferred_element_type=jnp.float32)


def per_device(tokens, gate_weight, up_weight, down_weight):
    width = gate_weight.shape[1]
    groups = lax.axis_size("gx")
    size = tokens.shape[0] // CHUNKS

    def project(part):
        part = gather_steps(part, 1, CORES)
        gate = dot(part, gate_weight).astype(jnp.bfloat16)
        up = dot(part, up_weight).astype(jnp.bfloat16)
        rows = part.shape[0] // groups
        return jnp.concatenate(
            [gate.reshape(groups, rows, width), up.reshape(groups, rows, width)], 2)

    def join(terms):
        summed = terms.astype(jnp.float32).sum(0)
        return (jax.nn.silu(summed[:, :width]) * summed[:, width:]).astype(jnp.bfloat16)

    def exchange(value):
        return lax.all_to_all(value, "gx", 0, 0)

    def spread(part):
        return exchange(jnp.broadcast_to(part[None], (groups,) + part.shape)).reshape(-1, width)

    def down(hidden):
        half = hidden.shape[0] // CORES
        came = swap(dot(hidden[half:], down_weight).astype(jnp.bfloat16), 1)
        mine = dot(hidden[:half], down_weight)
        return (mine + came.astype(jnp.float32)).astype(jnp.bfloat16)

    def over_z(value):
        return gather_steps(value, CORES, Z_PARTS)

    def over_y(value):
        return gather_steps(value, CORES * Z_PARTS, Y_PARTS)

    first, second = tokens[:size], tokens[size:]
    first = over_z(first)
    second = over_z(after(second, first))
    first = over_y(first)
    term_a = project(first)
    second = over_y(second)
    terms_a = exchange(term_a)
    hidden_a = join(terms_a)
    term_b = project(after(second, terms_a))
    all_a = spread(hidden_a)
    out_a = down(all_a)
    terms_b = exchange(after(term_b, all_a))
    out_a = reduce_steps(out_a, CORES * Z_PARTS, Y_PARTS)
    all_b = spread(join(terms_b))
    out_a = reduce_steps(out_a, CORES, Z_PARTS)
    out_b = down(all_b)
    out_b = reduce_steps(out_b, CORES * Z_PARTS, Y_PARTS)
    out_b = reduce_steps(out_b, CORES, Z_PARTS)
    return jnp.concatenate([out_a, out_b], 0)


def solution(mesh):
    in_specs = (P("gy", "gx"), P("gx", "gy"), P("gx", "gy"), P("gy", "gx"))
    out_specs = P("gy", "gx")
    return jax.shard_map(
        per_device, mesh=mesh, in_specs=in_specs, out_specs=out_specs, check_vma=False
    )
```

```python
import jax
import jax.numpy as jnp
from jax import lax
from jax.sharding import PartitionSpec as P

CORES, Z_PARTS, Y_PARTS = 2, 4, 4


def swap(value, step):
    size = CORES * Z_PARTS * Y_PARTS
    return lax.ppermute(value, "gy", [(a, a ^ step) for a in range(size)])


def gather_core(value):
    return jnp.concatenate([value, swap(value, 1)], 0)


def gather_ring(value, unit):
    half = value.shape[0] // 2
    left, right = swap(value, unit), swap(value, unit * 3)
    across = [swap(right[:half], unit), swap(left[half:], unit * 3)]
    return jnp.concatenate([value, left] + across + [right], 0)


def add(*values):
    return sum(value.astype(jnp.float32) for value in values).astype(jnp.bfloat16)


def reduce_ring(value, unit):
    rows = value.shape[0] // 4
    half = rows // 2
    mine, left, across, right = (value[i * rows:(i + 1) * rows] for i in range(4))
    for_right = swap(across[:half], unit)
    for_left = swap(across[half:], unit * 3)
    left = jnp.concatenate([left[:half], add(left[half:], for_left)], 0)
    right = jnp.concatenate([add(right[:half], for_right), right[half:]], 0)
    return add(mine, swap(left, unit), swap(right, unit * 3))


def per_device(tokens, gate_weight, up_weight, down_weight):
    width = gate_weight.shape[1]
    groups = lax.axis_size("gx")
    both = jnp.concatenate([gate_weight, up_weight], 1)
    part = gather_ring(tokens, CORES)
    part = gather_ring(part, CORES * Z_PARTS)
    part = gather_core(part)
    term = jnp.dot(part, both, preferred_element_type=jnp.float32).astype(jnp.bfloat16)
    rows = term.shape[0] // groups
    terms = lax.all_to_all(term.reshape(groups, rows, 2 * width), "gx", 0, 0)
    summed = terms.astype(jnp.float32).sum(0)
    hidden_part = (jax.nn.silu(summed[:, :width]) * summed[:, width:]).astype(jnp.bfloat16)
    hidden = lax.all_to_all(
        jnp.broadcast_to(hidden_part[None], (groups, rows, width)), "gx", 0, 0
    ).reshape(groups * rows, width)
    half = hidden.shape[0] // 2
    theirs = jnp.dot(hidden[half:], down_weight, preferred_element_type=jnp.float32).astype(jnp.bfloat16)
    came = swap(theirs, 1)
    mine = lax.optimization_barrier(
        jnp.dot(hidden[:half], down_weight, preferred_element_type=jnp.float32))
    out = (mine + came.astype(jnp.float32)).astype(jnp.bfloat16)
    out = reduce_ring(out, CORES * Z_PARTS)
    return reduce_ring(out, CORES)


def solution(mesh):
    in_specs = (P("gy", "gx"), P("gx", "gy"), P("gx", "gy"), P("gy", "gx"))
    out_specs = P("gy", "gx")
    return jax.shard_map(
        per_device, mesh=mesh, in_specs=in_specs, out_specs=out_specs, check_vma=False
    )
```

```python
import jax
import jax.numpy as jnp
from jax import lax
from jax.sharding import PartitionSpec as P

CORES, Z_PARTS, Y_PARTS = 2, 4, 4


SIZE = CORES * Z_PARTS * Y_PARTS
Z_THEN_Y = (CORES, CORES * Z_PARTS)


def swap(value, step):
    return lax.ppermute(value, "gy", [(a, a ^ step(a % CORES)) for a in range(SIZE)])


def ring_swap(value, place, i):
    return swap(value, lambda core: Z_THEN_Y[place ^ core] * i)


def core_swap(value):
    return swap(value, lambda core: 1)


def gather_ring(value, place):
    return jnp.concatenate([value] + [ring_swap(value, place, i) for i in range(1, Y_PARTS)], 0)


def reduce_ring(value, place):
    rows = value.shape[0] // Y_PARTS
    pieces = [value[i * rows:(i + 1) * rows] for i in range(Y_PARTS)]
    total = pieces[0].astype(jnp.float32)
    for i in range(1, Y_PARTS):
        total = total + ring_swap(pieces[i], place, i).astype(jnp.float32)
    return total.astype(jnp.bfloat16)


def per_device(tokens, gate_weight, up_weight, down_weight):
    width = gate_weight.shape[1]
    groups = lax.axis_size("gx")
    both = jnp.concatenate([gate_weight, up_weight], 1)
    part = gather_ring(tokens, 0)
    part = gather_ring(part, 1)
    part = jnp.concatenate([part, core_swap(part)], 0)
    term = jnp.dot(part, both, preferred_element_type=jnp.float32).astype(jnp.bfloat16)
    rows = term.shape[0] // groups
    terms = lax.all_to_all(term.reshape(groups, rows, 2 * width), "gx", 0, 0)
    summed = terms.astype(jnp.float32).sum(0)
    hidden_part = (jax.nn.silu(summed[:, :width]) * summed[:, width:]).astype(jnp.bfloat16)
    hidden = lax.all_to_all(
        jnp.broadcast_to(hidden_part[None], (groups, rows, width)), "gx", 0, 0
    ).reshape(groups * rows, width)
    half = hidden.shape[0] // 2
    theirs = jnp.dot(hidden[half:], down_weight, preferred_element_type=jnp.float32).astype(jnp.bfloat16)
    came = core_swap(theirs)
    mine = lax.optimization_barrier(
        jnp.dot(hidden[:half], down_weight, preferred_element_type=jnp.float32))
    out = (mine + came.astype(jnp.float32)).astype(jnp.bfloat16)
    out = reduce_ring(out, 1)
    return reduce_ring(out, 0)


def solution(mesh):
    in_specs = (P("gy", "gx"), P("gx", "gy"), P("gx", "gy"), P("gy", "gx"))
    out_specs = P("gy", "gx")
    return jax.shard_map(
        per_device, mesh=mesh, in_specs=in_specs, out_specs=out_specs, check_vma=False
    )
```

```python
import jax
import jax.numpy as jnp
from jax import lax
from jax.sharding import PartitionSpec as P

CORES, Z_PARTS, Y_PARTS = 2, 4, 4


SIZE = CORES * Z_PARTS * Y_PARTS
Z_STEP, Y_STEP = CORES, CORES * Z_PARTS
PAIRS = tuple((a * unit, (4 - a) * unit) for unit in (Z_STEP, Y_STEP) for a in (1, 3))


def swap(value, steps):
    return lax.ppermute(value, "gy", [(a, a ^ steps[a % CORES]) for a in range(SIZE)])


def core_swap(value):
    return swap(value, (1, 1))


def gather_pairs(value):
    for steps in PAIRS:
        value = jnp.concatenate([value, swap(value, steps)], 0)
    return value


def reduce_pairs(value):
    for steps in PAIRS[::-1]:
        half = value.shape[0] // 2
        came = swap(value[half:], steps)
        value = (value[:half].astype(jnp.float32) + came.astype(jnp.float32)).astype(jnp.bfloat16)
    return value


def per_device(tokens, gate_weight, up_weight, down_weight):
    width = gate_weight.shape[1]
    groups = lax.axis_size("gx")
    both = jnp.concatenate([gate_weight, up_weight], 1)
    part = gather_pairs(tokens)
    part = jnp.concatenate([part, core_swap(part)], 0)
    term = jnp.dot(part, both, preferred_element_type=jnp.float32).astype(jnp.bfloat16)
    rows = term.shape[0] // groups
    terms = lax.all_to_all(term.reshape(groups, rows, 2 * width), "gx", 0, 0)
    summed = terms.astype(jnp.float32).sum(0)
    hidden_part = (jax.nn.silu(summed[:, :width]) * summed[:, width:]).astype(jnp.bfloat16)
    hidden = lax.all_to_all(
        jnp.broadcast_to(hidden_part[None], (groups, rows, width)), "gx", 0, 0
    ).reshape(groups * rows, width)
    half = hidden.shape[0] // 2
    theirs = jnp.dot(hidden[half:], down_weight, preferred_element_type=jnp.float32).astype(jnp.bfloat16)
    came = core_swap(theirs)
    mine = lax.optimization_barrier(
        jnp.dot(hidden[:half], down_weight, preferred_element_type=jnp.float32))
    out = (mine + came.astype(jnp.float32)).astype(jnp.bfloat16)
    return reduce_pairs(out)


def solution(mesh):
    in_specs = (P("gy", "gx"), P("gx", "gy"), P("gx", "gy"), P("gy", "gx"))
    out_specs = P("gy", "gx")
    return jax.shard_map(
        per_device, mesh=mesh, in_specs=in_specs, out_specs=out_specs, check_vma=False
    )
```

```python
import jax
import jax.numpy as jnp
from jax import lax
from jax.sharding import PartitionSpec as P

CORES, Z_PARTS, Y_PARTS = 2, 4, 4


SIZE = CORES * Z_PARTS * Y_PARTS
Z_THEN_Y = (CORES, CORES * Z_PARTS)
NEAR_FIRST = (1, 3, 2)


def swap(value, step):
    return lax.ppermute(value, "gy", [(a, a ^ step(a % CORES)) for a in range(SIZE)])


def ring_swap(value, place, i):
    return swap(value, lambda core: Z_THEN_Y[place ^ core] * i)


def core_swap(value):
    return swap(value, lambda core: 1)


def gather_ring(value, place):
    return jnp.concatenate([value] + [ring_swap(value, place, i) for i in NEAR_FIRST], 0)


def reduce_ring(value, place, order):
    rows = value.shape[0] // Y_PARTS
    pieces = [value[i * rows:(i + 1) * rows] for i in range(Y_PARTS)]
    total = pieces[0].astype(jnp.float32)
    for i in order:
        total = total + ring_swap(pieces[1 + NEAR_FIRST.index(i)], place, i).astype(jnp.float32)
    return total.astype(jnp.bfloat16)


def per_device(tokens, gate_weight, up_weight, down_weight):
    width = gate_weight.shape[1]
    groups = lax.axis_size("gx")
    both = jnp.concatenate([gate_weight, up_weight], 1)
    part = gather_ring(tokens, 0)
    part = gather_ring(part, 1)
    part = jnp.concatenate([part, core_swap(part)], 0)
    term = jnp.dot(part, both, preferred_element_type=jnp.float32).astype(jnp.bfloat16)
    rows = term.shape[0] // groups
    terms = lax.all_to_all(term.reshape(groups, rows, 2 * width), "gx", 0, 0)
    summed = terms.astype(jnp.float32).sum(0)
    hidden_part = (jax.nn.silu(summed[:, :width]) * summed[:, width:]).astype(jnp.bfloat16)
    hidden = lax.all_to_all(
        jnp.broadcast_to(hidden_part[None], (groups, rows, width)), "gx", 0, 0
    ).reshape(groups * rows, width)
    half = hidden.shape[0] // 2
    theirs = jnp.dot(hidden[half:], down_weight, preferred_element_type=jnp.float32).astype(jnp.bfloat16)
    came = core_swap(theirs)
    mine = lax.optimization_barrier(
        jnp.dot(hidden[:half], down_weight, preferred_element_type=jnp.float32))
    out = (mine + came.astype(jnp.float32)).astype(jnp.bfloat16)
    out = reduce_ring(out, 1, (1, 2, 3))
    return reduce_ring(out, 0, NEAR_FIRST)


def solution(mesh):
    in_specs = (P("gy", "gx"), P("gx", "gy"), P("gx", "gy"), P("gy", "gx"))
    out_specs = P("gy", "gx")
    return jax.shard_map(
        per_device, mesh=mesh, in_specs=in_specs, out_specs=out_specs, check_vma=False
    )
```
